32 devices in a mesh: seq: 16 (over z, x, core), ch: 2 (over y).
Axes of the slice: x: 2, y: 2, z: 4, core: 2. Of those that a mesh axis runs over, the one named last changes fastest.
Arguments:
- projected: float32 [3, 32, 16, 2048], P(None, None, 'seq', 'ch'), may hold values from -6 to 6
- filter_taps: float32 [32, 16, 2048], P('ch', 'seq'), may hold values from -1.1 to 1.1
- skip_gain: float32 [32], P('ch'), may hold values from -4 to 4
Outputs:
- mixed: float32 [32, 16, 2048], P('ch', 'seq')
The draws below stay inside these ranges and needn't reach their ends.
All inputs are finite; a program needn't handle non-finite values.
Results may differ from the reference program's by a relative error of at most 0.00013.
Values sent between devices are 32-bit elements; how exact they have to be, the bound alone decides.
A program may use at most 64 MiB of HBM per device.

```python
import math
import jax
import jax.numpy as jnp

TOK_DEV = 2048
CH = 32
SEQ_LEN = 32768
N_SEQ = 16


def draw_filter_taps(key, part):
    key_rough = jax.random.fold_in(key, 11)
    key_rate = jax.random.fold_in(key, 12)
    key_kind = jax.random.fold_in(key, 13)
    key_fast = jax.random.fold_in(key, 14)
    key_tail = jax.random.fold_in(key, 15)
    key_share = jax.random.fold_in(key, 16)
    position = jnp.arange(SEQ_LEN, dtype=jnp.float32)[None, :]
    rough = jax.random.truncated_normal(key_rough, -3.5, 3.5, (CH, SEQ_LEN), jnp.float32)
    slow_share = 0.5
    chosen = jax.random.uniform(key_kind, (CH, 1), jnp.float32) < slow_share
    slow_rate = jnp.exp(jax.random.uniform(key_rate, (CH, 1), jnp.float32, math.log(0.2), math.log(2.0))) / SEQ_LEN
    fast_rate = jnp.exp(jax.random.uniform(key_fast, (CH, 1), jnp.float32, math.log(1.0 / 50.0), math.log(1.0 / 30.0)))
    rate = jnp.where(chosen, slow_rate, fast_rate)
    amplitude = jnp.sqrt(2.0 * rate + 1.0 / SEQ_LEN)
    tail_rate = jnp.exp(jax.random.uniform(key_tail, (CH, 1), jnp.float32, math.log(0.1), 0.0)) / SEQ_LEN
    tail_share = jnp.exp(jax.random.uniform(key_share, (CH, 1), jnp.float32, math.log(0.15), math.log(0.45)))
    tail_amplitude = jnp.sqrt(2.0 * tail_rate * tail_share)
    envelope = amplitude * jnp.exp(-rate * position) + tail_amplitude * jnp.exp(-tail_rate * position)
    taps = rough * envelope
    return jnp.swapaxes(taps.reshape(CH, TOK_DEV, SEQ_LEN // TOK_DEV), 1, 2)


def levels(stream_key, shape, cuts, smallest, largest):
    def one(dim, parts):
        heights = jax.random.uniform(jax.random.fold_in(jax.random.fold_in(stream_key, 6), dim), (parts,), jnp.float32, smallest / len(cuts), largest / len(cuts))
        return jnp.repeat(jnp.exp(heights), shape[dim] // parts).reshape((-1,) + (1,) * (len(shape) - dim - 1))

    loudness = one(*cuts[0])
    for cut in cuts[1:]:
        loudness = loudness * one(*cut)
    return loudness


def noise(own_key, shape, scale, reach, cuts=(), held_as=jnp.bfloat16):
    entries = scale * jax.random.normal(own_key, shape, jnp.float32)
    if cuts:
        entries = entries * levels(own_key, shape, cuts, -0.22, 0.18)
    return jnp.clip(entries, -reach, reach).astype(held_as)


def setup_inputs(seed: int = 0) -> dict:
    seeds = jax.random.split(jax.random.key(seed), 4)
    return {
        "projected": noise(seeds[0], (3, CH, N_SEQ, TOK_DEV), 1.0, 6.0, ((2, 16), (3, 2)), jnp.float32),
        "filter_taps": draw_filter_taps(jax.random.fold_in(seeds[3], 71), 0),
        "skip_gain": noise(seeds[2], (CH,), 1.0, 4.0, ((0, 2),), jnp.float32),
    }


def to_sequence(array):
    shape = array.shape
    lead = shape[:-2]
    moved = jnp.swapaxes(array, -1, -2)
    return moved.reshape(lead + (shape[-2] * shape[-1],))


def reference(projected, filter_taps, skip_gain):
    rows = to_sequence(projected)
    taps = to_sequence(filter_taps)
    value_row = rows[0]
    inner_gate = rows[1]
    outer_gate = rows[2]
    gated = inner_gate * value_row
    length_two = 2 * SEQ_LEN
    spec_in = jnp.fft.rfft(gated, n=length_two, axis=-1)
    spec_filter = jnp.fft.rfft(taps, n=length_two, axis=-1)
    conv = jnp.fft.irfft(spec_in * spec_filter, n=length_two, axis=-1)[:, :SEQ_LEN]
    result = outer_gate * (conv + skip_gain[:, None] * gated)
    return jnp.swapaxes(result.reshape(CH, TOK_DEV, N_SEQ), 1, 2)
```

```python
import functools

import jax
import jax.numpy as jnp
import numpy as np
from jax import lax
from jax.experimental import pallas as pl
from jax.experimental.pallas import tpu as pltpu
from jax.sharding import PartitionSpec as P

MESH = pl.DeviceIdType.MESH
LANES = 128
ROWS = 256


def split_np(table):
    high = table.astype(np.float32).astype(jnp.bfloat16)
    low = (table - high.astype(np.float64)).astype(np.float32).astype(jnp.bfloat16)
    return np.stack([high, low])


def tables(shards, tiles):
    order = 2 * tiles
    length = shards * LANES * order
    per_group = ROWS // tiles
    keys = LANES // shards
    ka = np.arange(tiles) + 0.5
    a = np.arange(tiles)
    angle = 2 * np.pi * np.outer(ka, a) / order
    eye = np.eye(per_group)
    first = np.concatenate(
        [
            np.einsum("ka,pq->kpqa", part, eye).reshape(tiles * per_group, ROWS)
            for part in (np.cos(angle), -np.sin(angle))
        ]
    )
    last = first.T * (2.0 / length)
    b = np.arange(LANES)
    angle = 2 * np.pi * (np.outer(b, b) % LANES) / LANES
    cosine, sine = np.cos(angle), np.sin(angle)
    lane = np.block([[cosine, -sine], [sine, cosine]])
    p = np.arange(shards)
    angle = 2 * np.pi * (np.outer(p, p) % shards) / shards
    cosine, sine = np.kron(np.eye(keys), np.cos(angle)), np.kron(np.eye(keys), np.sin(angle))
    shard = np.block([[cosine, sine], [-sine, cosine]])
    low = (p[:, None] + shards * b[None, :])[None]
    angle = -2 * np.pi * ka[:, None, None] * low / length
    angle = angle.reshape(tiles * shards, LANES)
    turn_one = np.stack([np.cos(angle), np.sin(angle)]).astype(np.float32)
    angle = -2 * np.pi * np.outer(p, b) / (LANES * shards)
    angle = np.tile(angle, (keys, 1))
    turn_two = np.stack([np.cos(angle), np.sin(angle)]).astype(np.float32)
    return (
        split_np(first),
        split_np(last),
        split_np(lane),
        split_np(shard),
        turn_one,
        turn_two,
    )


def parts_of(x):
    high = x.astype(jnp.bfloat16)
    low = (x - high.astype(jnp.float32)).astype(jnp.bfloat16)
    return high, low


def dot(left, right):
    return jnp.dot(left, right, preferred_element_type=jnp.float32)


def from_left(table, x):
    high, low = parts_of(x)
    return dot(table[0], high) + (dot(table[0], low) + dot(table[1], high))


def from_left_narrow(table, x):
    high, low = parts_of(x)
    both = dot(table[0], jnp.concatenate([high, low], axis=1))
    width = x.shape[1]
    return both[:, :width] + (both[:, width:] + dot(table[1], high))


def from_right(x, table):
    high, low = parts_of(x)
    return dot(high, table[0]) + (dot(low, table[0]) + dot(high, table[1]))


def convolve(gated, taps, shards, tiles, first, last, lane, shard, turn_one, turn_two):
    per_group = ROWS // tiles
    groups = shards // per_group
    rows = tiles * shards
    stages = []
    for g in range(groups):
        chosen = slice(g * ROWS, (g + 1) * ROWS)
        both = jnp.concatenate([gated[chosen], taps[chosen]], axis=1)
        stages.append(from_left(first, both))

    def rows_of(part, signal):
        pieces = [
            s[part * ROWS : (part + 1) * ROWS, signal * LANES : (signal + 1) * LANES] for s in stages
        ]
        if groups == 1:
            return pieces[0]
        pieces = [x.reshape(tiles, per_group, LANES) for x in pieces]
        return jnp.concatenate(pieces, axis=1).reshape(rows, LANES)

    one_re, one_im = turn_one[0], turn_one[1]
    two_re, two_im = turn_two[0], turn_two[1]
    spectra = []
    for signal in range(2):
        re, im = rows_of(0, signal), rows_of(1, signal)
        turned = jnp.concatenate([re * one_re - im * one_im, re * one_im + im * one_re], axis=1)
        spectra.append(from_right(turned, lane))
    backs = []
    for q in range(rows // LANES):
        chosen = slice(q * LANES, (q + 1) * LANES)
        res, ims = [], []
        for signal in range(2):
            re, im = spectra[signal][chosen, :LANES], spectra[signal][chosen, LANES:]
            res.append(re * two_re - im * two_im)
            ims.append(re * two_im + im * two_re)
        stacked = jnp.concatenate(
            [jnp.concatenate(res, axis=1), jnp.concatenate(ims, axis=1)], axis=0
        )
        full = from_left(shard, stacked)
        g_re, h_re = full[:LANES, :LANES], full[:LANES, LANES:]
        g_im, h_im = full[LANES:, :LANES], full[LANES:, LANES:]
        y_re = g_re * h_re - g_im * h_im
        y_im = g_re * h_im + g_im * h_re
        backs.append(jnp.concatenate([y_im, y_re], axis=0))
    turned = []
    for q in range(0, len(backs), 2):
        back = from_left(shard, jnp.concatenate(backs[q : q + 2], axis=1))
        for half in range(2):
            columns = slice(half * LANES, (half + 1) * LANES)
            re, im = back[LANES:, columns], back[:LANES, columns]
            turned.append(
                jnp.concatenate([im * two_re - re * two_im, re * two_re + im * two_im], axis=1)
            )
    back = from_right(jnp.concatenate(turned, axis=0), lane)
    re, im = back[:, LANES:], back[:, :LANES]
    out_re = re * one_re + im * one_im
    out_im = im * one_re - re * one_im
    results = []
    for g in range(groups):
        if groups == 1:
            stacked = jnp.concatenate([out_re, out_im], axis=0)
        else:
            part = slice(g * per_group, (g + 1) * per_group)
            stacked = jnp.concatenate(
                [
                    x.reshape(tiles, shards, LANES)[:, part].reshape(ROWS, LANES)
                    for x in (out_re, out_im)
                ],
                axis=0,
            )
        results.append(from_left_narrow(last, stacked))
    return results[0] if groups == 1 else jnp.concatenate(results, axis=0)


def far_first(count):
    return sorted(range(1, count), key=lambda d: (-min(d, count - d), d))


def kernel(
    shards, copies, channels, tiles,
    projected, taps, gain, *rest,
):
    table_refs, rest = rest[:6], rest[6:]
    out, rest = rest[0], rest[1:]
    held, rest = rest[:6], rest[6:]
    (
        inner, sending, g_in, h_in, outer, conv, y_in, gain_in,
        load_sem, table_sem, g_send, g_recv, h_send, h_recv, o_send, o_recv, y_send, y_recv,
    ) = rest
    me = lax.axis_index("seq")
    mine = lax.axis_index("ch")
    stride = shards // channels
    total = shards * copies
    rank = me * copies + mine

    barrier = pltpu.get_barrier_semaphore()
    for d in far_first(total):
        other = (rank + d) % total
        pl.semaphore_signal(
            barrier,
            inc=1,
            device_id={"seq": other // copies, "ch": other % copies},
            device_id_type=MESH,
        )
    load = pltpu.make_async_copy(projected.at[pl.ds(0, 2)], inner, load_sem.at[0])
    load.start()
    load_gain = pltpu.make_async_copy(gain, gain_in, load_sem.at[1])
    load_gain.start()
    loads = [
        pltpu.make_async_copy(table_refs[i], held[i], table_sem.at[i]) for i in range(6)
    ]
    for x in loads:
        x.start()
    load.wait()
    sending[...] = inner[0] * inner[1]
    pl.semaphore_wait(barrier, total - 1)

    owners = channels * copies
    own_slot = me // stride

    def send_gated(owner):
        index, target = owner // copies, owner % copies
        pltpu.make_async_remote_copy(
            src_ref=sending.at[target * channels + index],
            dst_ref=g_in.at[me, mine],
            send_sem=g_send,
            recv_sem=g_recv,
            device_id={"seq": index * stride, "ch": target},
            device_id_type=MESH,
        ).start()

    def send_taps(index):
        pltpu.make_async_remote_copy(
            src_ref=taps.at[index],
            dst_ref=h_in.at[me],
            send_sem=h_send,
            recv_sem=h_recv,
            device_id={"seq": index * stride, "ch": mine},
            device_id_type=MESH,
        ).start()

    is_owner = me % stride == 0
    own_channel = mine * channels + own_slot

    def when_owner(body):
        if stride == 1:
            body()
        else:
            pl.when(is_owner)(body)

    def when_not_owner(body):
        if stride > 1:
            pl.when(jnp.logical_not(is_owner))(body)

    for d in far_first(channels):
        send_taps((own_slot + d) % channels)
    own_rank = own_slot * copies + mine
    for d in far_first(owners):
        send_gated((own_rank + d) % owners)
    when_not_owner(lambda: send_gated(own_rank))
    when_not_owner(lambda: send_taps(own_slot))
    for d in range(1, copies):
        target = (mine + d) % copies
        pltpu.make_async_remote_copy(
            src_ref=projected.at[2, pl.ds(target * channels, channels)],
            dst_ref=outer.at[mine],
            send_sem=o_send,
            recv_sem=o_recv,
            device_id={"seq": me, "ch": target},
            device_id_type=MESH,
        ).start()
    pltpu.make_async_copy(
        projected.at[2, pl.ds(mine * channels, channels)], outer.at[mine], o_recv
    ).start()

    def own_blocks():
        pltpu.make_async_copy(sending.at[own_channel], g_in.at[me, mine], g_recv).start()
        pltpu.make_async_copy(taps.at[own_slot], h_in.at[me], h_recv).start()

    when_owner(own_blocks)
    load_gain.wait()
    for x in loads:
        x.wait()

    def transform():
        pltpu.make_async_copy(h_in, h_in, h_recv).wait()
        pltpu.make_async_copy(g_in, g_in, g_recv).wait()
        slab = gain_in[...]
        column = lax.broadcasted_iota(jnp.int32, slab.shape, 1)
        direct = jnp.sum(jnp.where(column == own_slot, slab, 0.0))
        signal = g_in[...].reshape(shards * tiles, LANES)
        filt = h_in[...].reshape(shards * tiles, LANES)
        row = lax.broadcasted_iota(jnp.int32, filt.shape, 0)
        column = lax.broadcasted_iota(jnp.int32, filt.shape, 1)
        filt = filt + jnp.where((row == 0) & (column == 0), direct, 0.0)
        result = convolve(signal, filt, shards, tiles, *held)
        conv[...] = result.reshape(shards, tiles, LANES)
        for d in far_first(shards):
            target = (me + d) % shards
            pltpu.make_async_remote_copy(
                src_ref=conv.at[target],
                dst_ref=y_in.at[own_slot],
                send_sem=y_send,
                recv_sem=y_recv,
                device_id={"seq": target, "ch": mine},
                device_id_type=MESH,
            ).start()
        pltpu.make_async_copy(conv.at[me], y_in.at[own_slot], y_recv).start()

    when_owner(transform)
    pltpu.make_async_copy(outer, outer, o_recv).wait()
    pltpu.make_async_copy(y_in, y_in, y_recv).wait()
    step = tiles // copies
    for c in range(copies):
        part = slice(c * step, (c + 1) * step)
        out[:, part] = y_in[:, part] * outer[c]

    def sent(ref, sem):
        pltpu.make_async_copy(ref, ref, sem).wait()

    def sent_by_owner():
        sent(conv.at[pl.ds(0, shards - 1)], y_send)
        sent(sending.at[pl.ds(0, owners - 1)], g_send)
        if channels > 1:
            sent(h_in.at[pl.ds(0, channels - 1)], h_send)

    def sent_by_other():
        sent(sending.at[pl.ds(0, owners)], g_send)
        sent(h_in.at[pl.ds(0, channels)], h_send)

    when_owner(sent_by_owner)
    when_not_owner(sent_by_other)
    if copies > 1:
        sent(outer.at[pl.ds(0, copies - 1)], o_send)


def on_device(shards, copies, projected, filter_taps, skip_gain):
    _, all_channels, _, part = projected.shape
    channels, _, length = filter_taps.shape
    tiles = length // LANES
    step = part // LANES
    constants = [jnp.asarray(x) for x in tables(shards, tiles)]
    any_spec = pl.BlockSpec(memory_space=pl.ANY)
    f32 = jnp.float32
    result = pl.pallas_call(
        functools.partial(kernel, shards, copies, channels, tiles),
        out_shape=jax.ShapeDtypeStruct((channels, tiles, LANES), f32),
        in_specs=[any_spec] * 9,
        out_specs=pl.BlockSpec(memory_space=pltpu.VMEM),
        scratch_shapes=[pltpu.VMEM(x.shape, x.dtype) for x in constants]
        + [
            pltpu.VMEM((2, all_channels, step, LANES), f32),
            pltpu.VMEM((all_channels, step, LANES), f32),
            pltpu.VMEM((shards, copies, step, LANES), f32),
            pltpu.VMEM((shards, tiles, LANES), f32),
            pltpu.VMEM((copies, channels, step, LANES), f32),
            pltpu.VMEM((shards, tiles, LANES), f32),
            pltpu.VMEM((channels, tiles, LANES), f32),
            pltpu.VMEM((1, channels), f32),
            pltpu.SemaphoreType.DMA((2,)),
            pltpu.SemaphoreType.DMA((6,)),
        ]
        + [pltpu.SemaphoreType.DMA] * 8,
        compiler_params=pltpu.CompilerParams(collective_id=0, has_side_effects=True),
    )(
        projected.reshape(3, all_channels, step, LANES),
        filter_taps.reshape(channels, tiles, LANES),
        skip_gain.reshape(1, channels),
        *constants,
    )
    return result.reshape(channels, 1, length)


def solution(mesh):
    return jax.shard_map(
        functools.partial(on_device, mesh.shape["seq"], mesh.shape["ch"]),
        mesh=mesh,
        in_specs=(P(None, None, "seq", "ch"), P("ch", "seq", None), P("ch")),
        out_specs=P("ch", "seq", None),
        check_vma=False,
    )
```

```python
import functools

import jax
import jax.numpy as jnp
import numpy as np
from jax import lax
from jax.experimental import pallas as pl
from jax.experimental.pallas import tpu as pltpu
from jax.sharding import PartitionSpec as P

MESH = pl.DeviceIdType.MESH
LANES = 128
ROWS = 256


def split_np(table):
    high = table.astype(np.float32).astype(jnp.bfloat16)
    low = (table - high.astype(np.float64)).astype(np.float32).astype(jnp.bfloat16)
    return np.stack([high, low])


def tables(shards, tiles):
    order = 2 * tiles
    length = shards * LANES * order
    per_group = ROWS // tiles
    keys = LANES // shards
    ka = np.arange(tiles) + 0.5
    a = np.arange(tiles)
    angle = 2 * np.pi * np.outer(ka, a) / order
    eye = np.eye(per_group)
    first = np.concatenate(
        [
            np.einsum("ka,pq->kpqa", part, eye).reshape(tiles * per_group, ROWS)
            for part in (np.cos(angle), -np.sin(angle))
        ]
    )
    last = first.T * (2.0 / length)
    b = np.arange(LANES)
    angle = 2 * np.pi * (np.outer(b, b) % LANES) / LANES
    cosine, sine = np.cos(angle), np.sin(angle)
    lane = np.block([[cosine, -sine], [sine, cosine]])
    p = np.arange(shards)
    angle = 2 * np.pi * (np.outer(p, p) % shards) / shards
    cosine, sine = np.kron(np.eye(keys), np.cos(angle)), np.kron(np.eye(keys), np.sin(angle))
    shard = np.block([[cosine, sine], [-sine, cosine]])
    low = (p[:, None] + shards * b[None, :])[None]
    angle = -2 * np.pi * ka[:, None, None] * low / length
    angle = angle.reshape(tiles * shards, LANES)
    turn_one = np.stack([np.cos(angle), np.sin(angle)]).astype(np.float32)
    angle = -2 * np.pi * np.outer(p, b) / (LANES * shards)
    angle = np.tile(angle, (keys, 1))
    turn_two = np.stack([np.cos(angle), np.sin(angle)]).astype(np.float32)
    return (
        split_np(first),
        split_np(last),
        split_np(lane),
        split_np(shard),
        turn_one,
        turn_two,
    )


def parts_of(x):
    high = x.astype(jnp.bfloat16)
    low = (x - high.astype(jnp.float32)).astype(jnp.bfloat16)
    return high, low


def dot(left, right):
    return jnp.dot(left, right, preferred_element_type=jnp.float32)


def from_left(table, x):
    high, low = parts_of(x)
    return dot(table[0], high) + (dot(table[0], low) + dot(table[1], high))


def from_left_narrow(table, x):
    high, low = parts_of(x)
    both = dot(table[0], jnp.concatenate([high, low], axis=1))
    width = x.shape[1]
    return both[:, :width] + (both[:, width:] + dot(table[1], high))


def from_right(x, table):
    high, low = parts_of(x)
    return dot(high, table[0]) + (dot(low, table[0]) + dot(high, table[1]))


def forward(signal, shards, tiles, first, lane, shard, turn_one, turn_two):
    per_group = ROWS // tiles
    groups = shards // per_group
    rows = tiles * shards
    stages = [
        from_left_narrow(first, signal[g * ROWS : (g + 1) * ROWS]) for g in range(groups)
    ]

    def rows_of(part):
        pieces = [s[part * ROWS : (part + 1) * ROWS] for s in stages]
        if groups == 1:
            return pieces[0]
        pieces = [x.reshape(tiles, per_group, LANES) for x in pieces]
        return jnp.concatenate(pieces, axis=1).reshape(rows, LANES)

    one_re, one_im = turn_one[0], turn_one[1]
    two_re, two_im = turn_two[0], turn_two[1]
    re, im = rows_of(0), rows_of(1)
    turned = jnp.concatenate([re * one_re - im * one_im, re * one_im + im * one_re], axis=1)
    spectrum = from_right(turned, lane)
    results = []
    for q in range(0, rows // LANES, 2):
        res, ims = [], []
        for half in range(2):
            chosen = slice((q + half) * LANES, (q + half + 1) * LANES)
            re, im = spectrum[chosen, :LANES], spectrum[chosen, LANES:]
            res.append(re * two_re - im * two_im)
            ims.append(re * two_im + im * two_re)
        stacked = jnp.concatenate(
            [jnp.concatenate(res, axis=1), jnp.concatenate(ims, axis=1)], axis=0
        )
        results.append(from_left(shard, stacked))
    return results


def backward(left, right, shards, tiles, lane, shard, turn_one, turn_two):
    per_group = ROWS // tiles
    groups = shards // per_group
    one_re, one_im = turn_one[0], turn_one[1]
    two_re, two_im = turn_two[0], turn_two[1]
    turned = []
    for g, h in zip(left, right):
        g_re, g_im, h_re, h_im = g[:LANES], g[LANES:], h[:LANES], h[LANES:]
        y_re = g_re * h_re - g_im * h_im
        y_im = g_re * h_im + g_im * h_re
        back = from_left(shard, jnp.concatenate([y_im, y_re], axis=0))
        for half in range(2):
            columns = slice(half * LANES, (half + 1) * LANES)
            re, im = back[LANES:, columns], back[:LANES, columns]
            turned.append(
                jnp.concatenate([im * two_re - re * two_im, re * two_re + im * two_im], axis=1)
            )
    back = from_right(jnp.concatenate(turned, axis=0), lane)
    re, im = back[:, LANES:], back[:, :LANES]
    parts = (re * one_re + im * one_im, im * one_re - re * one_im)
    if groups == 1:
        return [jnp.concatenate(parts, axis=0)]
    return [
        jnp.concatenate(
            [
                x.reshape(tiles, shards, LANES)[:, g * per_group : (g + 1) * per_group].reshape(
                    ROWS, LANES
                )
                for x in parts
            ],
            axis=0,
        )
        for g in range(groups)
    ]


def far_first(count):
    return sorted(range(1, count), key=lambda d: (-min(d, count - d), d))


def kernel(
    shards, copies, channels, tiles,
    projected, taps, gain, *rest,
):
    table_refs, rest = rest[:6], rest[6:]
    out, rest = rest[0], rest[1:]
    held, rest = rest[:6], rest[6:]
    (
        inner, sending, g_in, h_in, outer, conv, y_in, gain_in,
        load_sem, table_sem, g_send, g_recv, h_send, h_recv, o_send, o_recv, y_send, y_recv,
    ) = rest
    me = lax.axis_index("seq")
    mine = lax.axis_index("ch")
    stride = shards // channels
    total = shards * copies
    rank = me * copies + mine

    barrier = pltpu.get_barrier_semaphore()
    for d in far_first(total):
        other = (rank + d) % total
        pl.semaphore_signal(
            barrier,
            inc=1,
            device_id={"seq": other // copies, "ch": other % copies},
            device_id_type=MESH,
        )
    load = pltpu.make_async_copy(projected.at[pl.ds(0, 2)], inner, load_sem.at[0])
    load.start()
    load_gain = pltpu.make_async_copy(gain, gain_in, load_sem.at[1])
    load_gain.start()
    loads = [
        pltpu.make_async_copy(table_refs[i], held[i], table_sem.at[i]) for i in range(6)
    ]
    for x in loads:
        x.start()
    load.wait()
    sending[...] = inner[0] * inner[1]
    pl.semaphore_wait(barrier, total - 1)

    owners = channels * copies
    own_slot = me // stride

    def send_gated(owner):
        index, target = owner // copies, owner % copies
        pltpu.make_async_remote_copy(
            src_ref=sending.at[target * channels + index],
            dst_ref=g_in.at[me, mine],
            send_sem=g_send,
            recv_sem=g_recv,
            device_id={"seq": index * stride, "ch": target},
            device_id_type=MESH,
        ).start()

    def send_taps(index):
        pltpu.make_async_remote_copy(
            src_ref=taps.at[index],
            dst_ref=h_in.at[me],
            send_sem=h_send,
            recv_sem=h_recv,
            device_id={"seq": index * stride, "ch": mine},
            device_id_type=MESH,
        ).start()

    is_owner = me % stride == 0
    own_channel = mine * channels + own_slot

    def when_owner(body):
        if stride == 1:
            body()
        else:
            pl.when(is_owner)(body)

    def when_not_owner(body):
        if stride > 1:
            pl.when(jnp.logical_not(is_owner))(body)

    for d in far_first(channels):
        send_taps((own_slot + d) % channels)
    own_rank = own_slot * copies + mine
    for d in far_first(owners):
        send_gated((own_rank + d) % owners)
    when_not_owner(lambda: send_gated(own_rank))
    when_not_owner(lambda: send_taps(own_slot))
    for d in range(1, copies):
        target = (mine + d) % copies
        pltpu.make_async_remote_copy(
            src_ref=projected.at[2, pl.ds(target * channels, channels)],
            dst_ref=outer.at[mine],
            send_sem=o_send,
            recv_sem=o_recv,
            device_id={"seq": me, "ch": target},
            device_id_type=MESH,
        ).start()
    pltpu.make_async_copy(
        projected.at[2, pl.ds(mine * channels, channels)], outer.at[mine], o_recv
    ).start()

    def own_blocks():
        pltpu.make_async_copy(sending.at[own_channel], g_in.at[me, mine], g_recv).start()
        pltpu.make_async_copy(taps.at[own_slot], h_in.at[me], h_recv).start()

    when_owner(own_blocks)
    load_gain.wait()
    for x in loads:
        x.wait()

    def transform():
        first, last, lane, shard, turn_one, turn_two = held
        pltpu.make_async_copy(h_in, h_in, h_recv).wait()
        slab = gain_in[...]
        column = lax.broadcasted_iota(jnp.int32, slab.shape, 1)
        direct = jnp.sum(jnp.where(column == own_slot, slab, 0.0))
        filt = h_in[...].reshape(shards * tiles, LANES)
        row = lax.broadcasted_iota(jnp.int32, filt.shape, 0)
        column = lax.broadcasted_iota(jnp.int32, filt.shape, 1)
        filt = filt + jnp.where((row == 0) & (column == 0), direct, 0.0)
        right = forward(filt, shards, tiles, first, lane, shard, turn_one, turn_two)
        pltpu.make_async_copy(g_in, g_in, g_recv).wait()
        signal = g_in[...].reshape(shards * tiles, LANES)
        left = forward(signal, shards, tiles, first, lane, shard, turn_one, turn_two)
        stacks = backward(left, right, shards, tiles, lane, shard, turn_one, turn_two)

        def send_result(target):
            pltpu.make_async_remote_copy(
                src_ref=conv.at[target],
                dst_ref=y_in.at[own_slot],
                send_sem=y_send,
                recv_sem=y_recv,
                device_id={"seq": target, "ch": mine},
                device_id_type=MESH,
            ).start()

        if len(stacks) == 1:
            half = shards // 2
            high, low = parts_of(stacks[0])
            both = jnp.concatenate([high, low], axis=1)
            for turn in range(2):
                base = (me // half + 1 + turn) % 2 * half
                chosen = pl.ds(pl.multiple_of(base * tiles, half * tiles), half * tiles)
                wide = dot(last[0, chosen], both)
                result = wide[:, :LANES] + (wide[:, LANES:] + dot(last[1, chosen], high))
                conv[pl.ds(base, half)] = result.reshape(half, tiles, LANES)
                for d in range(turn, half):
                    send_result(base + (me + d) % half)
        else:
            results = [from_left_narrow(last, x) for x in stacks]
            conv[...] = jnp.concatenate(results, axis=0).reshape(shards, tiles, LANES)
            for d in far_first(shards):
                send_result((me + d) % shards)
        pltpu.make_async_copy(conv.at[me], y_in.at[own_slot], y_recv).start()

    when_owner(transform)
    pltpu.make_async_copy(outer, outer, o_recv).wait()
    pltpu.make_async_copy(y_in, y_in, y_recv).wait()
    step = tiles // copies
    for c in range(copies):
        part = slice(c * step, (c + 1) * step)
        out[:, part] = y_in[:, part] * outer[c]

    def sent(ref, sem):
        pltpu.make_async_copy(ref, ref, sem).wait()

    def sent_by_owner():
        sent(conv.at[pl.ds(0, shards - 1)], y_send)
        sent(sending.at[pl.ds(0, owners - 1)], g_send)
        if channels > 1:
            sent(h_in.at[pl.ds(0, channels - 1)], h_send)

    def sent_by_other():
        sent(sending.at[pl.ds(0, owners)], g_send)
        sent(h_in.at[pl.ds(0, channels)], h_send)

    when_owner(sent_by_owner)
    when_not_owner(sent_by_other)
    if copies > 1:
        sent(outer.at[pl.ds(0, copies - 1)], o_send)


def on_device(shards, copies, projected, filter_taps, skip_gain):
    _, all_channels, _, part = projected.shape
    channels, _, length = filter_taps.shape
    tiles = length // LANES
    step = part // LANES
    constants = [jnp.asarray(x) for x in tables(shards, tiles)]
    any_spec = pl.BlockSpec(memory_space=pl.ANY)
    f32 = jnp.float32
    result = pl.pallas_call(
        functools.partial(kernel, shards, copies, channels, tiles),
        out_shape=pltpu.VMEM((channels, tiles, LANES), f32),
        in_specs=[any_spec] * 9,
        out_specs=pl.BlockSpec(memory_space=pltpu.VMEM),
        scratch_shapes=[pltpu.VMEM(x.shape, x.dtype) for x in constants]
        + [
            pltpu.VMEM((2, all_channels, step, LANES), f32),
            pltpu.VMEM((all_channels, step, LANES), f32),
            pltpu.VMEM((shards, copies, step, LANES), f32),
            pltpu.VMEM((shards, tiles, LANES), f32),
            pltpu.VMEM((copies, channels, step, LANES), f32),
            pltpu.VMEM((shards, tiles, LANES), f32),
            pltpu.VMEM((channels, tiles, LANES), f32),
            pltpu.VMEM((1, channels), f32),
            pltpu.SemaphoreType.DMA((2,)),
            pltpu.SemaphoreType.DMA((6,)),
        ]
        + [pltpu.SemaphoreType.DMA] * 8,
        compiler_params=pltpu.CompilerParams(collective_id=0, has_side_effects=True),
    )(
        projected.reshape(3, all_channels, step, LANES),
        filter_taps.reshape(channels, tiles, LANES),
        skip_gain.reshape(1, channels),
        *constants,
    )
    return result.reshape(channels, 1, length)


def solution(mesh):
    return jax.shard_map(
        functools.partial(on_device, mesh.shape["seq"], mesh.shape["ch"]),
        mesh=mesh,
        in_specs=(P(None, None, "seq", "ch"), P("ch", "seq", None), P("ch")),
        out_specs=P("ch", "seq", None),
        check_vma=False,
    )
```
